32 devices in a mesh: band: 2 (over x), blk: 16 (over z, y, core).
Axes of the slice: x: 2, y: 2, z: 4, core: 2. Of those that a mesh axis runs over, the one named last changes fastest.
Arguments:
- spectra: bfloat16 [768, 4, 1024], P(('band', 'blk')), parts along dimension 0, may hold values from -6 to 6
- counts: int32 [768, 4], P(('band', 'blk')), parts along dimension 0, may hold values from 0 to 12
Outputs:
- correlograms: bfloat16 [768, 16, 1024], P(('band', 'blk')), parts along dimension 0
The draws below stay inside these ranges and needn't reach their ends.
There are 2 independent parts, one for each index of `band`. The reference program is written for one: setup_inputs(seed, part) draws one part's arguments, and reference() takes and returns one part's arrays. A program takes and returns all parts, laid end to end along the dimension named above; each array names one. Nothing has to cross between parts.
All inputs are finite; a program needn't handle non-finite values.
Results may differ from the reference program's by a relative error of at most 0.0085.
Values may be sent and summed in bfloat16 or wider, within the bound.
A program may use at most 64 MiB of HBM per device.

```python
import math
import jax
import jax.numpy as jnp
from jax import lax

STA_DEV = 24
SEG = 4
LAG = 1024
WINS = 12
NF = 512
STATIONS = 384
N_BLK = 16


def touch_ends(array, key, smallest, top_value):
    index_at = [jax.random.randint(jax.random.fold_in(key, axis), (), 0, length) for axis, length in enumerate(array.shape)]
    main_axis = array.shape.index(max(array.shape))
    next_to = index_at[:main_axis] + [(index_at[main_axis] + 1) % array.shape[main_axis]] + index_at[main_axis + 1:]
    return array.at[tuple(index_at)].set(smallest).at[tuple(next_to)].set(top_value)


def block_levels(rng, extent, shards, least, top_value):
    def one(dim, shards_of):
        steps = jax.random.uniform(jax.random.fold_in(jax.random.fold_in(rng, 6), dim), (shards_of,), jnp.float32, least / len(shards), top_value / len(shards))
        return jnp.repeat(jnp.exp(steps), extent[dim] // shards_of).reshape((-1,) + (1,) * (len(extent) - dim - 1))

    loudness = one(*shards[0])
    for cut in shards[1:]:
        loudness = loudness * one(*cut)
    return loudness


def scatter_about(stream_key, dims, deviation, limit, pieces=(), held_as=jnp.bfloat16):
    values = jax.random.normal(stream_key, dims, jnp.float32) * deviation
    if len(pieces) > 0:
        values = block_levels(stream_key, dims, pieces, -0.22, 0.18) * values
    return jnp.clip(values, min=-limit, max=limit).astype(held_as)


def setup_inputs(seed: int = 0, part: int = 0) -> dict:
    key_list = jax.random.split(jax.random.key(seed), 3)
    own_keys = jax.random.split(jax.random.fold_in(key_list[2], part), 3)
    spectra = scatter_about(own_keys[0], (STATIONS, SEG, 2 * NF), 1.0, 6.0, ((0, 16),))
    counts = touch_ends(jax.random.randint(own_keys[1], (STATIONS, SEG), 0, WINS + 1), jax.random.fold_in(own_keys[1], 1), 0, WINS).astype(jnp.int32)
    return dict(spectra=spectra, counts=counts)


def lag_table():
    bins = jnp.arange(LAG // 2, dtype=jnp.int32)
    taps = jnp.arange(LAG, dtype=jnp.int32) - LAG // 2
    phase = bins[:, None] * taps[None, :] % LAG
    angle = phase.astype(jnp.float32) * (2.0 * math.pi / LAG)
    return jnp.concatenate([jnp.cos(angle), jnp.sin(angle)], 0).astype(jnp.bfloat16)

def split_parts(block, block_counts):
    half = block.shape[2] // 2
    real_part = block[:, :, :half].astype(jnp.float32)
    imag_part = block[:, :, half:].astype(jnp.float32)
    inverse = lax.rsqrt(real_part * real_part + imag_part * imag_part + 0.25)
    return (real_part, imag_part, real_part * inverse, imag_part * inverse, block_counts.astype(jnp.float32))

def pair_beams(own, own_counts, other, other_counts):
    ra, ia, pa, qa, ca = split_parts(own, own_counts)
    rb, ib, pb, qb, cb = split_parts(other, other_counts)
    acc_re = 0.0
    acc_im = 0.0
    coh_re = 0.0
    coh_im = 0.0
    weight_sum = 0.0
    for seg in range(ra.shape[1]):
        weight = jnp.minimum(ca[:, None, seg], cb[None, :, seg])[:, :, None]
        xa_re = ra[:, None, seg, :]
        xa_im = ia[:, None, seg, :]
        xb_re = rb[None, :, seg, :]
        xb_im = ib[None, :, seg, :]
        acc_re = acc_re + weight * (xa_re * xb_re + xa_im * xb_im)
        acc_im = acc_im + weight * (xa_im * xb_re - xa_re * xb_im)
        ya_re = pa[:, None, seg, :]
        ya_im = qa[:, None, seg, :]
        yb_re = pb[None, :, seg, :]
        yb_im = qb[None, :, seg, :]
        coh_re = coh_re + weight * (ya_re * yb_re + ya_im * yb_im)
        coh_im = coh_im + weight * (ya_im * yb_re - ya_re * yb_im)
        weight_sum = weight_sum + weight
    total = jnp.maximum(weight_sum, 1.0)
    factor = (coh_re * coh_re + coh_im * coh_im) / (total * total * total)
    stack_re = acc_re * factor
    stack_im = acc_im * factor
    forward = jnp.concatenate([lax.optimization_barrier(jnp.sum(stack_re, 1)), lax.optimization_barrier(jnp.sum(stack_im, 1))], -1)
    backward = jnp.concatenate([lax.optimization_barrier(jnp.sum(stack_re, 0)), -lax.optimization_barrier(jnp.sum(stack_im, 0))], -1)
    return (forward, backward)

def reference(spectra, counts):
    table = lag_table()
    blocks = spectra.reshape(N_BLK, STA_DEV, SEG, spectra.shape[2])
    block_counts = counts.reshape(N_BLK, STA_DEV, SEG)

    def per_source(source):

        def per_offset(offset):
            target = (source + offset) % N_BLK
            forward, unused = pair_beams(blocks[source], block_counts[source], blocks[target], block_counts[target])
            return forward.astype(jnp.bfloat16)
        beam = lax.map(per_offset, jnp.arange(N_BLK, dtype=jnp.int32))
        traces = jnp.dot(beam.reshape(-1, beam.shape[2]), table, preferred_element_type=jnp.float32).astype(jnp.bfloat16)
        values = traces.astype(jnp.float32).reshape(N_BLK, STA_DEV, LAG)
        scale = jnp.sqrt(lax.optimization_barrier(jnp.mean(values * values, -1, keepdims=True)) + 1e-06)
        return jnp.transpose((values / scale).astype(jnp.bfloat16), (1, 0, 2))
    result = lax.map(per_source, jnp.arange(N_BLK, dtype=jnp.int32))
    return result.reshape(N_BLK * STA_DEV, N_BLK, LAG)
```

```python
import functools
import math

import jax
import jax.numpy as jnp
from jax import lax
from jax.experimental import pallas as pl
from jax.experimental.pallas import tpu as pltpu
from jax.sharding import PartitionSpec as P

LAG = 1024
LANES = 128
ROWS = 8


def lag_table():
    fine = 16
    taps = jnp.arange(LAG, dtype=jnp.int32) - LAG // 2

    def small(bins):
        phase = bins[:, None] * taps[None, :] % LAG
        angle = phase.astype(jnp.float32) * (2.0 * math.pi / LAG)
        return lax.optimization_barrier((jnp.cos(angle), jnp.sin(angle)))

    c0, s0 = small(jnp.arange(fine, dtype=jnp.int32))
    c1, s1 = small(jnp.arange(LAG // 2 // fine, dtype=jnp.int32) * fine)
    cos = c1[:, None] * c0[None] - s1[:, None] * s0[None]
    sin = s1[:, None] * c0[None] + c1[:, None] * s0[None]
    both = jnp.concatenate([cos.reshape(-1, LAG), sin.reshape(-1, LAG)], 0)
    return both.astype(jnp.bfloat16)


def chip_of(place, chips, snake):
    if not snake:
        return place
    return jnp.where(place < chips // 2, 2 * place, 2 * (chips - 1 - place) + 1)


def place_of(chip, chips, snake):
    if not snake:
        return chip
    return jnp.where(chip % 2 == 0, chip // 2, chips - 1 - chip // 2)


def unpack(block, half):
    re = block[:, :half].astype(jnp.float32)
    im = block[:, half : 2 * half].astype(jnp.float32)
    count = block[:, 2 * half :].astype(jnp.float32)
    return re, im, lax.rsqrt(re * re + im * im + 0.25), count


def pair_kernel(
    n, snake, own_ref, beam_ref, slots, mine, seen, parts, back, back_out,
    fwd_send, fwd_recv, sib_send, sib_recv, back_send, back_recv,
):
    segs, stations, width = own_ref.shape
    half = (width - LANES) // 2
    chips = n // 2
    far = chips // 2
    band = lax.axis_index("band")
    me = lax.axis_index("blk")
    core = me % 2
    place = place_of(me // 2, chips, snake)

    def device(where, which):
        return chip_of(where % chips, chips, snake) * 2 + which

    left = device(place + chips - 1, core)
    sibling = device(place, 1 - core)

    barrier = pltpu.get_barrier_semaphore()
    for step in range(1, n):
        pl.semaphore_signal(
            barrier, inc=1, device_id=(band, (me + step) % n),
            device_id_type=pl.DeviceIdType.MESH,
        )
    pl.semaphore_wait(barrier, n - 1)

    def send_left(hop, source):
        return pltpu.make_async_remote_copy(
            src_ref=source, dst_ref=slots.at[2 * hop], send_sem=fwd_send.at[hop],
            recv_sem=fwd_recv.at[hop], device_id=(band, left),
            device_id_type=pl.DeviceIdType.MESH,
        )

    def send_sibling(hop, source):
        return pltpu.make_async_remote_copy(
            src_ref=source, dst_ref=slots.at[2 * hop + 1], send_sem=sib_send.at[hop],
            recv_sem=sib_recv.at[hop], device_id=(band, sibling),
            device_id_type=pl.DeviceIdType.MESH,
        )

    def send_back(slot, other):
        return pltpu.make_async_remote_copy(
            src_ref=back_out.at[slot], dst_ref=beam_ref.at[(me + n - other) % n],
            send_sem=back_send.at[slot], recv_sem=back_recv.at[slot],
            device_id=(band, other), device_id_type=pl.DeviceIdType.MESH,
        )

    send_left(1, own_ref).start()
    send_sibling(0, own_ref).start()

    for seg in range(segs):
        re, im, inv, count = unpack(own_ref[seg], half)
        for i in range(stations):
            for at, value in ((0, re), (half, im), (2 * half, inv), (3 * half, count)):
                size = value.shape[1]
                mine[i, seg, :, at : at + size] = jnp.broadcast_to(value[i : i + 1], (ROWS, size))

    def unit(block_ref, with_back):
        for seg in range(segs):
            re, im, inv, count = unpack(block_ref[seg], half)
            seen[seg, :, :half] = re
            seen[seg, :, half : 2 * half] = im
            seen[seg, :, 2 * half : 3 * half] = inv
            seen[seg, :, 3 * half :] = count
        if with_back:
            back[...] = jnp.zeros_like(back)

        def station(i, carry):
            weights = []
            for r in range(0, stations, ROWS):
                w = [
                    jnp.minimum(mine[i, s, :, 3 * half :], seen[s, r : r + ROWS, 3 * half :])
                    for s in range(segs)
                ]
                total = jnp.maximum(functools.reduce(jnp.add, w), 1.0)
                share = 1.0 / total
                weights.append([v * share for v in w])
            for c in range(0, half, LANES):
                own = [
                    [mine[i, s, :, at + c : at + c + LANES] for at in (0, half, 2 * half)]
                    for s in range(segs)
                ]
                ahead_re = ahead_im = None
                for index, r in enumerate(range(0, stations, ROWS)):
                    cross_re = cross_im = coh_re = coh_im = None
                    for s in range(segs):
                        ar, ai, ag = own[s]
                        br, bi, bg = [
                            seen[s, r : r + ROWS, at + c : at + c + LANES]
                            for at in (0, half, 2 * half)
                        ]
                        w = weights[index][s]
                        x = w * (ar * br + ai * bi)
                        y = w * (ai * br - ar * bi)
                        g = ag * bg
                        if s == 0:
                            cross_re, cross_im, coh_re, coh_im = x, y, g * x, g * y
                        else:
                            cross_re = cross_re + x
                            cross_im = cross_im + y
                            coh_re = coh_re + g * x
                            coh_im = coh_im + g * y
                    factor = coh_re * coh_re + coh_im * coh_im
                    stack_re = cross_re * factor
                    stack_im = cross_im * factor
                    if with_back:
                        back[r : r + ROWS, c : c + LANES] += stack_re
                        back[r : r + ROWS, half + c : half + c + LANES] -= stack_im
                    ahead_re = stack_re if index == 0 else ahead_re + stack_re
                    ahead_im = stack_im if index == 0 else ahead_im + stack_im
                parts[i, :, c : c + LANES] = ahead_re
                parts[i, :, half + c : half + c + LANES] = ahead_im
            return carry

        lax.fori_loop(0, stations, station, 0)

    def finish(other):
        beam_ref[(other + n - me) % n] = jnp.sum(parts[...], 1).astype(jnp.bfloat16)

    def return_back(slot, other):
        back_out[slot] = back[...].astype(jnp.bfloat16)
        send_back(slot, other).start()

    unit(own_ref, False)
    finish(me)
    send_left(1, own_ref).wait_recv()
    if far > 1:
        send_left(2, slots.at[2]).start()
    send_sibling(1, slots.at[2]).start()
    send_sibling(0, own_ref).wait_recv()
    unit(slots.at[1], False)
    finish(sibling)

    def stage(hop, carry):
        other = device(place + hop, core)
        unit(slots.at[2 * hop], True)
        finish(other)
        return_back(2 * hop, other)
        send_left(hop + 1, own_ref).wait_recv()

        @pl.when(hop + 1 < far)
        def _():
            send_left(hop + 2, slots.at[2 * hop + 2]).start()

        send_sibling(hop + 1, slots.at[2 * hop + 2]).start()
        other = device(place + hop, 1 - core)
        send_sibling(hop, own_ref).wait_recv()
        unit(slots.at[2 * hop + 1], True)
        finish(other)
        return_back(2 * hop + 1, other)
        return carry

    lax.fori_loop(1, far, stage, 0)
    send_sibling(far, own_ref).wait_recv()
    low = place < far
    pick = jnp.where(low, 0, 1)
    other = device(place + far, jnp.where(low, core, 1 - core))
    unit(slots.at[2 * far + pick], True)
    finish(other)
    return_back(2 * far, other)

    def drain(hop, carry):
        send_left(hop, own_ref).wait_send()
        send_sibling(hop, own_ref).wait_send()
        return carry

    send_sibling(0, own_ref).wait_send()
    lax.fori_loop(1, far + 1, drain, 0)

    def drain_back(slot, carry):
        send_back(slot, sibling).wait()
        return carry

    lax.fori_loop(2, 2 * far + 1, drain_back, 0)


def pair_beams(packed, n, snake):
    segs, stations, width = packed.shape
    half = (width - LANES) // 2
    far = n // 4
    dma = pltpu.SemaphoreType.DMA
    pairs = (n // 2 + 1) * stations * stations * half
    return pl.pallas_call(
        functools.partial(pair_kernel, n, snake),
        out_shape=jax.ShapeDtypeStruct((n, stations, 2 * half), jnp.bfloat16),
        in_specs=[pl.BlockSpec(memory_space=pltpu.VMEM)],
        out_specs=pl.BlockSpec(memory_space=pltpu.VMEM),
        scratch_shapes=[
            pltpu.VMEM((2 * far + 2, segs, stations, width), jnp.bfloat16),
            pltpu.VMEM((stations, segs, ROWS, 3 * half + LANES), jnp.float32),
            pltpu.VMEM((segs, stations, 3 * half + LANES), jnp.float32),
            pltpu.VMEM((stations, ROWS, 2 * half), jnp.float32),
            pltpu.VMEM((stations, 2 * half), jnp.float32),
            pltpu.VMEM((2 * far + 1, stations, 2 * half), jnp.bfloat16),
            dma((far + 1,)), dma((far + 1,)), dma((far + 1,)), dma((far + 1,)),
            dma((2 * far + 1,)), dma((2 * far + 1,)),
        ],
        compiler_params=pltpu.CompilerParams(
            collective_id=0, has_side_effects=True, vmem_limit_bytes=48 * 1024 * 1024
        ),
        cost_estimate=pl.CostEstimate(
            flops=66 * pairs, bytes_accessed=2 * packed.size, transcendentals=0
        ),
        name="pair_beams",
    )(packed)


def shards(snake, spectra, counts):
    n = lax.axis_size("blk")
    stations, segs, spread = spectra.shape
    splat = jnp.broadcast_to(counts.astype(jnp.bfloat16)[:, :, None], (stations, segs, LANES))
    packed = jnp.concatenate([spectra, splat], 2).transpose(1, 0, 2)
    beams = pair_beams(packed, n, snake)
    table = lag_table()
    rows = jnp.dot(beams.reshape(-1, spread), table, preferred_element_type=jnp.float32)
    values = rows.astype(jnp.bfloat16).astype(jnp.float32)
    scale = jnp.sqrt(jnp.mean(values * values, -1, keepdims=True) + 1e-06)
    out = (values / scale).astype(jnp.bfloat16)
    return out.reshape(n, stations, LAG).transpose(1, 0, 2)


def solution(mesh):
    snake = mesh.shape["blk"] == 16
    return jax.shard_map(
        functools.partial(shards, snake),
        mesh=mesh,
        in_specs=(P(("band", "blk"), None, None), P(("band", "blk"), None)),
        out_specs=P(("band", "blk"), None, None),
        check_vma=False,
    )
```

```python
import functools
import math

import jax
import jax.numpy as jnp
from jax import lax
from jax.experimental import pallas as pl
from jax.experimental.pallas import tpu as pltpu
from jax.sharding import PartitionSpec as P

LAG = 1024
WINS = 12
LANES = 128
ROWS = 8


def lag_table():
    fine = 16
    taps = jnp.arange(LAG, dtype=jnp.int32) - LAG // 2

    def small(bins):
        phase = bins[:, None] * taps[None, :] % LAG
        angle = phase.astype(jnp.float32) * (2.0 * math.pi / LAG)
        return lax.optimization_barrier((jnp.cos(angle), jnp.sin(angle)))

    c0, s0 = small(jnp.arange(fine, dtype=jnp.int32))
    c1, s1 = small(jnp.arange(LAG // 2 // fine, dtype=jnp.int32) * fine)
    cos = c1[:, None] * c0[None] - s1[:, None] * s0[None]
    sin = s1[:, None] * c0[None] + c1[:, None] * s0[None]
    cos, sin = cos.reshape(2, -1, LAG), sin.reshape(2, -1, LAG)
    both = jnp.concatenate([cos[0], sin[0], cos[1], sin[1]], 0)
    return both.astype(jnp.bfloat16)


def chip_of(place, chips, snake):
    if not snake:
        return place
    return jnp.where(place < chips // 2, 2 * place, 2 * (chips - 1 - place) + 1)


def place_of(chip, chips, snake):
    if not snake:
        return chip
    return jnp.where(chip % 2 == 0, chip // 2, chips - 1 - chip // 2)


def pair_kernel(
    n, snake, levels, own_ref, splat_ref, flat_ref, beam_ref, slots, table, weight, norm, seen,
    ahead, parts, back_out, counts_in, counts, fwd_send, fwd_recv, sib_send, sib_recv,
    back_send, back_recv, count_send, count_recv, local_sem,
):
    rows, width = own_ref.shape[1:]
    stations = beam_ref.shape[2]
    segs = rows // stations
    part = width // 2
    chips = n // 2
    far = chips // 2
    band = lax.axis_index("band")
    me = lax.axis_index("blk")
    core = me % 2
    place = place_of(me // 2, chips, snake)
    low = place < far
    mesh_id = pl.DeviceIdType.MESH

    def device(where, which):
        return chip_of(where % chips, chips, snake) * 2 + which

    left = device(place + chips - 1, core)
    right = device(place + 1, core)
    sibling = device(place, 1 - core)
    ways = ((0, left), (1, right))

    barrier = pltpu.get_barrier_semaphore()
    for step in range(1, n):
        pl.semaphore_signal(barrier, inc=1, device_id=(band, (me + step) % n), device_id_type=mesh_id)
    pl.semaphore_wait(barrier, n - 1)

    def hand_on(way, hop, source, target):
        return pltpu.make_async_remote_copy(
            src_ref=source, dst_ref=slots.at[way, 2 * hop], send_sem=fwd_send.at[way, hop],
            recv_sem=fwd_recv.at[way, hop], device_id=(band, target), device_id_type=mesh_id,
        )

    def share(way, hop, source):
        return pltpu.make_async_remote_copy(
            src_ref=source, dst_ref=slots.at[way, 2 * hop + 1], send_sem=sib_send.at[way, hop],
            recv_sem=sib_recv.at[way, hop], device_id=(band, sibling), device_id_type=mesh_id,
        )

    def give_back(way, slot, other):
        return pltpu.make_async_remote_copy(
            src_ref=back_out.at[way, slot], dst_ref=beam_ref.at[way, (me + n - other) % n],
            send_sem=back_send.at[way, slot], recv_sem=back_recv.at[way, slot],
            device_id=(band, other), device_id_type=mesh_id,
        )

    def tell(step):
        return pltpu.make_async_remote_copy(
            src_ref=flat_ref, dst_ref=counts_in.at[me], send_sem=count_send.at[step],
            recv_sem=count_recv.at[step], device_id=(band, (me + step) % n), device_id_type=mesh_id,
        )

    for step in range(1, n):
        tell(step).start()
    for way, target in ways:
        hand_on(way, 1, own_ref.at[way], target).start()
    share(1 - core, 0, own_ref.at[1 - core]).start()

    def unpack(block):
        re = block[:, :part].astype(jnp.float32)
        im = block[:, part:].astype(jnp.float32)
        return re, im, lax.rsqrt(re * re + im * im + 0.25)

    counts_in[me] = flat_ref[...]
    for way in range(2):
        re, im, inv = unpack(own_ref[way])
        norm[way] = inv
        for level in range(levels):
            held = jnp.minimum(splat_ref[...], float(level))
            if way == 0:
                weight[level] = held
            for c in range(0, part, LANES):
                table[way, level, :, c : c + LANES] = held * re[:, c : c + LANES]
                table[way, level, :, part + c : part + c + LANES] = held * im[:, c : c + LANES]
    for step in range(1, n):
        tell(step).wait()
    to_scalars = pltpu.make_async_copy(counts_in, counts, local_sem)
    to_scalars.start()
    to_scalars.wait()

    def unit(way, block_ref, other, slot):
        re, im, inv = unpack(block_ref[...])
        for c in range(0, part, LANES):
            seen[c // LANES] = re[:, c : c + LANES]
            seen[(part + c) // LANES] = im[:, c : c + LANES]
            seen[(2 * part + c) // LANES] = inv[:, c : c + LANES]
        ahead[...] = jnp.zeros_like(ahead)

        def station(j, carry):
            level = [counts[other, 0, j * segs + s] for s in range(segs)]
            shares = []
            for r in range(0, stations, ROWS):
                total = functools.reduce(
                    jnp.add,
                    [
                        weight[level[s], s * stations + r : s * stations + r + ROWS, :]
                        for s in range(segs)
                    ],
                )
                one = 1.0 / jnp.maximum(total, 1.0)
                shares.append(one * one * one)
            for c in range(0, part, LANES):
                theirs = [
                    [
                        seen[(at + c) // LANES, pl.ds(s * stations + j, ROWS, stride=0), :]
                        for at in (0, part, 2 * part)
                    ]
                    for s in range(segs)
                ]
                behind_re = behind_im = None
                for index, r in enumerate(range(0, stations, ROWS)):
                    cross_re = cross_im = coh_re = coh_im = None
                    for s in range(segs):
                        at = s * stations + r
                        ar = table[way, level[s], at : at + ROWS, c : c + LANES]
                        ai = table[way, level[s], at : at + ROWS, part + c : part + c + LANES]
                        ag = norm[way, at : at + ROWS, c : c + LANES]
                        br, bi, bg = theirs[s]
                        x = ar * br + ai * bi
                        y = ai * br - ar * bi
                        g = ag * bg
                        if s == 0:
                            cross_re, cross_im, coh_re, coh_im = x, y, g * x, g * y
                        else:
                            cross_re = cross_re + x
                            cross_im = cross_im + y
                            coh_re = coh_re + g * x
                            coh_im = coh_im + g * y
                    factor = (coh_re * coh_re + coh_im * coh_im) * shares[index]
                    stack_re = cross_re * factor
                    stack_im = cross_im * factor
                    ahead[r : r + ROWS, c : c + LANES] += stack_re
                    ahead[r : r + ROWS, part + c : part + c + LANES] += stack_im
                    behind_re = stack_re if index == 0 else behind_re + stack_re
                    behind_im = stack_im if index == 0 else behind_im + stack_im
                if slot is not None:
                    parts[j, :, c : c + LANES] = behind_re
                    parts[j, :, part + c : part + c + LANES] = -behind_im
            return carry

        lax.fori_loop(0, stations, station, 0)
        beam_ref[way, (other + n - me) % n] = ahead[...].astype(jnp.bfloat16)
        if slot is not None:
            back_out[way, slot] = jnp.sum(parts[...], 1).astype(jnp.bfloat16)
            give_back(way, slot, other).start()

    def own_unit(way, carry):
        unit(way, own_ref.at[way], me, None)
        return carry

    lax.fori_loop(0, 2, own_unit, 0)

    def pass_on(hop):
        for way, target in ways:
            here = slots.at[way, 2 * hop]
            hand_on(way, hop, here, target).wait_recv()
            wanted = (hop + 1 < far) | ((hop + 1 == far) & last_wanted[way])

            @pl.when(wanted)
            def _():
                hand_on(way, hop + 1, here, target).start()

            share(way, hop, here).start()

    last_wanted = (
        (place + chips - 1) % chips < far,
        (place + 1) % chips >= far,
    )
    last_way = jnp.where(low, 0, 1)

    pass_on(1)
    share(core, 0, own_ref.at[core]).wait_recv()
    unit(core, slots.at[core, 1], sibling, 1)

    def stage(hop, carry):
        def both(way, carry):
            where = place + jnp.where(way == 0, hop, chips - hop)
            unit(way, slots.at[way, 2 * hop], device(where, core), 2 * hop)
            return carry

        def both_shared(way, carry):
            where = place + jnp.where(way == 0, hop, chips - hop)
            share(way, hop, own_ref.at[way]).wait_recv()
            unit(way, slots.at[way, 2 * hop + 1], device(where, 1 - core), 2 * hop + 1)
            return carry

        lax.fori_loop(0, 2, both, 0)

        @pl.when(hop + 1 < far)
        def _():
            pass_on(hop + 1)

        @pl.when(hop + 1 == far)
        def _():
            here = slots.at[last_way, 2 * far]
            hand_on(last_way, far, here, left).wait_recv()
            share(last_way, far, here).start()

        lax.fori_loop(0, 2, both_shared, 0)
        return carry

    lax.fori_loop(1, far, stage, 0)
    unit(last_way, slots.at[last_way, 2 * far], device(place + far, core), 2 * far)
    share(last_way, far, own_ref.at[0]).wait_recv()
    unit(last_way, slots.at[last_way, 2 * far + 1], device(place + far, 1 - core), 2 * far + 1)

    share(1 - core, 0, own_ref.at[0]).wait_send()
    share(last_way, far, own_ref.at[0]).wait_send()
    give_back(core, 1, sibling).wait_send()
    give_back(1 - core, 1, sibling).wait_recv()
    for which in range(2):
        give_back(last_way, 2 * far + which, sibling).wait_send()
        give_back(1 - last_way, 2 * far + which, sibling).wait_recv()
    for way, target in ways:

        def drain(hop, carry):
            hand_on(way, hop, own_ref.at[0], target).wait_send()
            share(way, hop, own_ref.at[0]).wait_send()
            give_back(way, 2 * hop, sibling).wait()
            give_back(way, 2 * hop + 1, sibling).wait()
            return carry

        lax.fori_loop(1, far, drain, 0)

        @pl.when(last_wanted[way])
        def _():
            hand_on(way, far, own_ref.at[0], target).wait_send()


def pair_beams(packed, splat, flat, n, snake, levels):
    _, rows, width = packed.shape
    segs = 4
    stations = rows // segs
    part = width // 2
    far = n // 4
    dma = pltpu.SemaphoreType.DMA
    pairs = (n // 2 + 1) * stations * stations * 2 * part
    vmem = pl.BlockSpec(memory_space=pltpu.VMEM)
    return pl.pallas_call(
        functools.partial(pair_kernel, n, snake, levels),
        out_shape=jax.ShapeDtypeStruct((2, n, stations, width), jnp.bfloat16),
        in_specs=[vmem, vmem, vmem],
        out_specs=vmem,
        scratch_shapes=[
            pltpu.VMEM((2, 2 * far + 2, rows, width), jnp.bfloat16),
            pltpu.VMEM((2, levels, rows, width), jnp.float32),
            pltpu.VMEM((levels, rows, LANES), jnp.float32),
            pltpu.VMEM((2, rows, part), jnp.float32),
            pltpu.VMEM((3 * part // LANES, rows, LANES), jnp.float32),
            pltpu.VMEM((stations, width), jnp.float32),
            pltpu.VMEM((stations, ROWS, width), jnp.float32),
            pltpu.VMEM((2, 2 * far + 2, stations, width), jnp.bfloat16),
            pltpu.VMEM((n, 1, LANES), jnp.int32),
            pltpu.SMEM((n, 1, LANES), jnp.int32),
            dma((2, far + 1)), dma((2, far + 1)), dma((2, far + 1)), dma((2, far + 1)),
            dma((2, 2 * far + 2)), dma((2, 2 * far + 2)), dma((n,)), dma((n,)), dma,
        ],
        compiler_params=pltpu.CompilerParams(
            collective_id=0, has_side_effects=True, vmem_limit_bytes=56 * 1024 * 1024
        ),
        cost_estimate=pl.CostEstimate(
            flops=60 * pairs, bytes_accessed=2 * packed.size, transcendentals=0
        ),
        name="pair_beams",
    )(packed, splat, flat)


def shards(snake, spectra, counts):
    n = lax.axis_size("blk")
    stations, segs, spread = spectra.shape
    packed = spectra.reshape(stations, segs, 2, 2, spread // 4).transpose(3, 1, 0, 2, 4)
    packed = packed.reshape(2, segs * stations, spread // 2)
    splat = jnp.broadcast_to(
        counts.astype(jnp.float32).T.reshape(-1, 1), (segs * stations, LANES)
    )
    flat = jnp.pad(counts.reshape(1, -1), ((0, 0), (0, LANES - counts.size)))
    beams = pair_beams(packed, splat, flat, n, snake, WINS + 1)
    table = lag_table()
    halves = beams.reshape(2, n * stations, spread // 2)
    rows = jnp.dot(halves[0], table[: spread // 2], preferred_element_type=jnp.float32)
    rows += jnp.dot(halves[1], table[spread // 2 :], preferred_element_type=jnp.float32)
    values = rows.astype(jnp.bfloat16).astype(jnp.float32)
    scale = jnp.sqrt(jnp.mean(values * values, -1, keepdims=True) + 1e-06)
    out = (values / scale).astype(jnp.bfloat16)
    return out.reshape(n, stations, LAG).transpose(1, 0, 2)


def solution(mesh):
    snake = mesh.shape["blk"] == 16
    return jax.shard_map(
        functools.partial(shards, snake),
        mesh=mesh,
        in_specs=(P(("band", "blk"), None, None), P(("band", "blk"), None)),
        out_specs=P(("band", "blk"), None, None),
        check_vma=False,
    )
```

```python
import functools
import math

import jax
import jax.numpy as jnp
from jax import lax
from jax.experimental import pallas as pl
from jax.experimental.pallas import tpu as pltpu
from jax.sharding import PartitionSpec as P

LAG = 1024
LANES = 128
ROWS = 8


def lag_table():
    fine = 16
    taps = jnp.arange(LAG, dtype=jnp.int32) - LAG // 2

    def small(bins):
        phase = bins[:, None] * taps[None, :] % LAG
        angle = phase.astype(jnp.float32) * (2.0 * math.pi / LAG)
        return lax.optimization_barrier((jnp.cos(angle), jnp.sin(angle)))

    c0, s0 = small(jnp.arange(fine, dtype=jnp.int32))
    c1, s1 = small(jnp.arange(LAG // 2 // fine, dtype=jnp.int32) * fine)
    cos = c1[:, None] * c0[None] - s1[:, None] * s0[None]
    sin = s1[:, None] * c0[None] + c1[:, None] * s0[None]
    both = jnp.concatenate([cos.reshape(-1, LAG), sin.reshape(-1, LAG)], 0)
    return both.astype(jnp.bfloat16)


def chip_of(place, chips, snake):
    if not snake:
        return place
    return jnp.where(place < chips // 2, 2 * place, 2 * (chips - 1 - place) + 1)


def place_of(chip, chips, snake):
    if not snake:
        return chip
    return jnp.where(chip % 2 == 0, chip // 2, chips - 1 - chip // 2)


def unpack(block, half):
    re = block[:, :half].astype(jnp.float32)
    im = block[:, half : 2 * half].astype(jnp.float32)
    count = block[:, 2 * half :].astype(jnp.float32)
    return re, im, lax.rsqrt(re * re + im * im + 0.25), count


def pair_kernel(
    n, snake, own_ref, beam_ref, slots, mine, seen, parts, back, back_out,
    fwd_send, fwd_recv, sib_send, sib_recv, back_send, back_recv,
):
    segs, stations, width = own_ref.shape
    half = (width - LANES) // 2
    chips = n // 2
    far = chips // 2
    band = lax.axis_index("band")
    me = lax.axis_index("blk")
    core = me % 2
    place = place_of(me // 2, chips, snake)

    def device(where, which):
        return chip_of(where % chips, chips, snake) * 2 + which

    left = device(place + chips - 1, core)
    sibling = device(place, 1 - core)

    barrier = pltpu.get_barrier_semaphore()
    for step in range(1, n):
        pl.semaphore_signal(
            barrier, inc=1, device_id=(band, (me + step) % n),
            device_id_type=pl.DeviceIdType.MESH,
        )
    pl.semaphore_wait(barrier, n - 1)

    def send_left(hop, source):
        return pltpu.make_async_remote_copy(
            src_ref=source, dst_ref=slots.at[2 * hop], send_sem=fwd_send.at[hop],
            recv_sem=fwd_recv.at[hop], device_id=(band, left),
            device_id_type=pl.DeviceIdType.MESH,
        )

    def send_sibling(hop, source):
        return pltpu.make_async_remote_copy(
            src_ref=source, dst_ref=slots.at[2 * hop + 1], send_sem=sib_send.at[hop],
            recv_sem=sib_recv.at[hop], device_id=(band, sibling),
            device_id_type=pl.DeviceIdType.MESH,
        )

    def send_back(slot, other):
        return pltpu.make_async_remote_copy(
            src_ref=back_out.at[slot], dst_ref=beam_ref.at[(me + n - other) % n],
            send_sem=back_send.at[slot], recv_sem=back_recv.at[slot],
            device_id=(band, other), device_id_type=pl.DeviceIdType.MESH,
        )

    send_left(1, own_ref).start()
    send_sibling(0, own_ref).start()

    for seg in range(segs):
        re, im, inv, count = unpack(own_ref[seg], half)
        for i in range(stations):
            for at, value in ((0, re), (half, im), (2 * half, inv), (3 * half, count)):
                size = value.shape[1]
                mine[i, seg, :, at : at + size] = jnp.broadcast_to(value[i : i + 1], (ROWS, size))

    def unit(block_ref, with_back):
        for seg in range(segs):
            re, im, inv, count = unpack(block_ref[seg], half)
            seen[seg, :, :half] = re
            seen[seg, :, half : 2 * half] = im
            seen[seg, :, 2 * half : 3 * half] = inv
            seen[seg, :, 3 * half :] = count
        if with_back:
            back[...] = jnp.zeros_like(back)

        def station(i, carry):
            weights = []
            for r in range(0, stations, ROWS):
                w = [
                    jnp.minimum(mine[i, s, :, 3 * half :], seen[s, r : r + ROWS, 3 * half :])
                    for s in range(segs)
                ]
                total = jnp.maximum(functools.reduce(jnp.add, w), 1.0)
                share = 1.0 / total
                weights.append([v * share for v in w])
            for c in range(0, half, LANES):
                own = [
                    [mine[i, s, :, at + c : at + c + LANES] for at in (0, half, 2 * half)]
                    for s in range(segs)
                ]
                ahead_re = ahead_im = None
                for index, r in enumerate(range(0, stations, ROWS)):
                    cross_re = cross_im = coh_re = coh_im = None
                    for s in range(segs):
                        ar, ai, ag = own[s]
                        br, bi, bg = [
                            seen[s, r : r + ROWS, at + c : at + c + LANES]
                            for at in (0, half, 2 * half)
                        ]
                        w = weights[index][s]
                        x = w * (ar * br + ai * bi)
                        y = w * (ai * br - ar * bi)
                        g = ag * bg
                        if s == 0:
                            cross_re, cross_im, coh_re, coh_im = x, y, g * x, g * y
                        else:
                            cross_re = cross_re + x
                            cross_im = cross_im + y
                            coh_re = coh_re + g * x
                            coh_im = coh_im + g * y
                    factor = coh_re * coh_re + coh_im * coh_im
                    stack_re = cross_re * factor
                    stack_im = cross_im * factor
                    if with_back:
                        back[r : r + ROWS, c : c + LANES] += stack_re
                        back[r : r + ROWS, half + c : half + c + LANES] -= stack_im
                    ahead_re = stack_re if index == 0 else ahead_re + stack_re
                    ahead_im = stack_im if index == 0 else ahead_im + stack_im
                parts[i, :, c : c + LANES] = ahead_re
                parts[i, :, half + c : half + c + LANES] = ahead_im
            return carry

        lax.fori_loop(0, stations, station, 0, unroll=2)

    def finish(other):
        beam_ref[(other + n - me) % n] = jnp.sum(parts[...], 1).astype(jnp.bfloat16)

    def return_back(slot, other):
        back_out[slot] = back[...].astype(jnp.bfloat16)
        send_back(slot, other).start()

    unit(own_ref, False)
    finish(me)
    send_left(1, own_ref).wait_recv()
    if far > 1:
        send_left(2, slots.at[2]).start()
    send_sibling(1, slots.at[2]).start()

    def stage(hop, carry):
        other = device(place + hop, core)
        unit(slots.at[2 * hop], True)
        finish(other)
        return_back(2 * hop, other)
        send_left(hop + 1, own_ref).wait_recv()

        @pl.when(hop + 1 < far)
        def _():
            send_left(hop + 2, slots.at[2 * hop + 2]).start()

        send_sibling(hop + 1, slots.at[2 * hop + 2]).start()
        other = device(place + hop, 1 - core)
        send_sibling(hop, own_ref).wait_recv()
        unit(slots.at[2 * hop + 1], True)
        finish(other)
        return_back(2 * hop + 1, other)
        return carry

    lax.fori_loop(1, far, stage, 0)
    send_sibling(far, own_ref).wait_recv()
    low = place < far
    pick = jnp.where(low, 0, 1)
    other = device(place + far, jnp.where(low, core, 1 - core))
    unit(slots.at[2 * far + pick], True)
    finish(other)
    return_back(2 * far, other)

    send_sibling(0, own_ref).wait_recv()
    unit(slots.at[1], False)
    finish(sibling)

    def drain(hop, carry):
        send_left(hop, own_ref).wait_send()
        send_sibling(hop, own_ref).wait_send()
        return carry

    send_sibling(0, own_ref).wait_send()
    lax.fori_loop(1, far + 1, drain, 0)

    def drain_back(slot, carry):
        send_back(slot, sibling).wait()
        return carry

    lax.fori_loop(2, 2 * far + 1, drain_back, 0)


def pair_beams(packed, n, snake):
    segs, stations, width = packed.shape
    half = (width - LANES) // 2
    far = n // 4
    dma = pltpu.SemaphoreType.DMA
    pairs = (n // 2 + 1) * stations * stations * half
    return pl.pallas_call(
        functools.partial(pair_kernel, n, snake),
        out_shape=jax.ShapeDtypeStruct((n, stations, 2 * half), jnp.bfloat16),
        in_specs=[pl.BlockSpec(memory_space=pltpu.VMEM)],
        out_specs=pl.BlockSpec(memory_space=pltpu.VMEM),
        scratch_shapes=[
            pltpu.VMEM((2 * far + 2, segs, stations, width), jnp.bfloat16),
            pltpu.VMEM((stations, segs, ROWS, 3 * half + LANES), jnp.float32),
            pltpu.VMEM((segs, stations, 3 * half + LANES), jnp.float32),
            pltpu.VMEM((stations, ROWS, 2 * half), jnp.float32),
            pltpu.VMEM((stations, 2 * half), jnp.float32),
            pltpu.VMEM((2 * far + 1, stations, 2 * half), jnp.bfloat16),
            dma((far + 1,)), dma((far + 1,)), dma((far + 1,)), dma((far + 1,)),
            dma((2 * far + 1,)), dma((2 * far + 1,)),
        ],
        compiler_params=pltpu.CompilerParams(
            collective_id=0, has_side_effects=True, vmem_limit_bytes=48 * 1024 * 1024
        ),
        cost_estimate=pl.CostEstimate(
            flops=66 * pairs, bytes_accessed=2 * packed.size, transcendentals=0
        ),
        name="pair_beams",
    )(packed)


def shards(snake, spectra, counts):
    n = lax.axis_size("blk")
    stations, segs, spread = spectra.shape
    splat = jnp.broadcast_to(counts.astype(jnp.bfloat16)[:, :, None], (stations, segs, LANES))
    packed = jnp.concatenate([spectra, splat], 2).transpose(1, 0, 2)
    beams = pair_beams(packed, n, snake)
    table = lag_table()
    rows = jnp.dot(beams.reshape(-1, spread), table, preferred_element_type=jnp.float32)
    values = rows.astype(jnp.bfloat16).astype(jnp.float32)
    scale = jnp.sqrt(jnp.mean(values * values, -1, keepdims=True) + 1e-06)
    out = (values / scale).astype(jnp.bfloat16)
    return out.reshape(n, stations, LAG).transpose(1, 0, 2)


def solution(mesh):
    snake = mesh.shape["blk"] == 16
    return jax.shard_map(
        functools.partial(shards, snake),
        mesh=mesh,
        in_specs=(P(("band", "blk"), None, None), P(("band", "blk"), None)),
        out_specs=P(("band", "blk"), None, None),
        check_vma=False,
    )
```

```python
import functools
import math

import jax
import jax.numpy as jnp
from jax import lax
from jax.experimental import pallas as pl
from jax.experimental.pallas import tpu as pltpu
from jax.sharding import PartitionSpec as P

LAG = 1024
SEGS = 4
LANES = 128
ROWS = 8


def lag_table():
    fine = 16
    taps = jnp.arange(LAG, dtype=jnp.int32) - LAG // 2

    def small(bins):
        phase = bins[:, None] * taps[None, :] % LAG
        angle = phase.astype(jnp.float32) * (2.0 * math.pi / LAG)
        return lax.optimization_barrier((jnp.cos(angle), jnp.sin(angle)))

    c0, s0 = small(jnp.arange(fine, dtype=jnp.int32))
    c1, s1 = small(jnp.arange(LAG // 2 // fine, dtype=jnp.int32) * fine)
    cos = c1[:, None] * c0[None] - s1[:, None] * s0[None]
    sin = s1[:, None] * c0[None] + c1[:, None] * s0[None]
    both = jnp.concatenate([cos.reshape(-1, LAG), sin.reshape(-1, LAG)], 0)
    return both.astype(jnp.bfloat16)


def chip_of(place, chips, snake):
    if not snake:
        return place
    return jnp.where(place < chips // 2, 2 * place, 2 * (chips - 1 - place) + 1)


def place_of(chip, chips, snake):
    if not snake:
        return chip
    return jnp.where(chip % 2 == 0, chip // 2, chips - 1 - chip // 2)


def unpack(block_ref, seg, segs, half):
    base = seg * 2 * half
    last = segs * 2 * half
    re = block_ref[:, base : base + half].astype(jnp.float32)
    im = block_ref[:, base + half : base + 2 * half].astype(jnp.float32)
    count = block_ref[:, last : last + LANES].astype(jnp.float32)[:, seg : seg + 1]
    count = jnp.broadcast_to(count, (re.shape[0], LANES))
    return re, im, lax.rsqrt(re * re + im * im + 0.25), count


def pair_kernel(
    n, snake, own_ref, beam_ref, slots, mine, seen, parts, back, back_out,
    fwd_send, fwd_recv, sib_send, sib_recv, back_send, back_recv,
):
    stations, width = own_ref.shape
    segs = SEGS
    half = (width - LANES) // (2 * segs)
    chips = n // 2
    far = chips // 2
    band = lax.axis_index("band")
    me = lax.axis_index("blk")
    core = me % 2
    place = place_of(me // 2, chips, snake)

    def device(where, which):
        return chip_of(where % chips, chips, snake) * 2 + which

    left = device(place + chips - 1, core)
    sibling = device(place, 1 - core)

    barrier = pltpu.get_barrier_semaphore()
    for step in range(1, n):
        pl.semaphore_signal(
            barrier, inc=1, device_id=(band, (me + step) % n),
            device_id_type=pl.DeviceIdType.MESH,
        )
    pl.semaphore_wait(barrier, n - 1)

    def send_left(hop, source):
        return pltpu.make_async_remote_copy(
            src_ref=source, dst_ref=slots.at[2 * hop], send_sem=fwd_send.at[hop],
            recv_sem=fwd_recv.at[hop], device_id=(band, left),
            device_id_type=pl.DeviceIdType.MESH,
        )

    def send_sibling(hop, source):
        return pltpu.make_async_remote_copy(
            src_ref=source, dst_ref=slots.at[2 * hop + 1], send_sem=sib_send.at[hop],
            recv_sem=sib_recv.at[hop], device_id=(band, sibling),
            device_id_type=pl.DeviceIdType.MESH,
        )

    def send_back(slot, other):
        return pltpu.make_async_remote_copy(
            src_ref=back_out.at[slot], dst_ref=beam_ref.at[(me + n - other) % n],
            send_sem=back_send.at[slot], recv_sem=back_recv.at[slot],
            device_id=(band, other), device_id_type=pl.DeviceIdType.MESH,
        )

    send_left(1, own_ref).start()
    send_sibling(0, own_ref).start()

    for seg in range(segs):
        re, im, inv, count = unpack(own_ref, seg, segs, half)
        for i in range(stations):
            for at, value in ((0, re), (half, im), (2 * half, inv), (3 * half, count)):
                size = value.shape[1]
                mine[i, seg, :, at : at + size] = jnp.broadcast_to(value[i : i + 1], (ROWS, size))

    def unit(block_ref, with_back):
        for seg in range(segs):
            re, im, inv, count = unpack(block_ref, seg, segs, half)
            seen[seg, :, :half] = re
            seen[seg, :, half : 2 * half] = im
            seen[seg, :, 2 * half : 3 * half] = inv
            seen[seg, :, 3 * half :] = count
        if with_back:
            back[...] = jnp.zeros_like(back)

        def station(i, carry):
            weights = []
            for r in range(0, stations, ROWS):
                w = [
                    jnp.minimum(mine[i, s, :, 3 * half :], seen[s, r : r + ROWS, 3 * half :])
                    for s in range(segs)
                ]
                total = jnp.maximum(functools.reduce(jnp.add, w), 1.0)
                share = 1.0 / total
                weights.append([v * share for v in w])
            for c in range(0, half, LANES):
                own = [
                    [mine[i, s, :, at + c : at + c + LANES] for at in (0, half, 2 * half)]
                    for s in range(segs)
                ]
                ahead_re = ahead_im = None
                for index, r in enumerate(range(0, stations, ROWS)):
                    cross_re = cross_im = coh_re = coh_im = None
                    for s in range(segs):
                        ar, ai, ag = own[s]
                        br, bi, bg = [
                            seen[s, r : r + ROWS, at + c : at + c + LANES]
                            for at in (0, half, 2 * half)
                        ]
                        w = weights[index][s]
                        x = w * (ar * br + ai * bi)
                        y = w * (ai * br - ar * bi)
                        g = ag * bg
                        if s == 0:
                            cross_re, cross_im, coh_re, coh_im = x, y, g * x, g * y
                        else:
                            cross_re = cross_re + x
                            cross_im = cross_im + y
                            coh_re = coh_re + g * x
                            coh_im = coh_im + g * y
                    factor = coh_re * coh_re + coh_im * coh_im
                    stack_re = cross_re * factor
                    stack_im = cross_im * factor
                    if with_back:
                        back[r : r + ROWS, c : c + LANES] += stack_re
                        back[r : r + ROWS, half + c : half + c + LANES] -= stack_im
                    ahead_re = stack_re if index == 0 else ahead_re + stack_re
                    ahead_im = stack_im if index == 0 else ahead_im + stack_im
                parts[i, :, c : c + LANES] = ahead_re
                parts[i, :, half + c : half + c + LANES] = ahead_im
            return carry

        lax.fori_loop(0, stations, station, 0, unroll=2)

    def finish(other):
        beam_ref[(other + n - me) % n] = jnp.sum(parts[...], 1).astype(jnp.bfloat16)

    def return_back(slot, other):
        back_out[slot] = back[...].astype(jnp.bfloat16)
        send_back(slot, other).start()

    unit(own_ref, False)
    finish(me)
    send_left(1, own_ref).wait_recv()
    if far > 1:
        send_left(2, slots.at[2]).start()
    send_sibling(1, slots.at[2]).start()

    def stage(hop, carry):
        other = device(place + hop, core)
        unit(slots.at[2 * hop], True)
        finish(other)
        return_back(2 * hop, other)
        send_left(hop + 1, own_ref).wait_recv()

        @pl.when(hop + 1 < far)
        def _():
            send_left(hop + 2, slots.at[2 * hop + 2]).start()

        send_sibling(hop + 1, slots.at[2 * hop + 2]).start()
        other = device(place + hop, 1 - core)
        send_sibling(hop, own_ref).wait_recv()
        unit(slots.at[2 * hop + 1], True)
        finish(other)
        return_back(2 * hop + 1, other)
        return carry

    lax.fori_loop(1, far, stage, 0)
    send_sibling(far, own_ref).wait_recv()
    low = place < far
    pick = jnp.where(low, 0, 1)
    other = device(place + far, jnp.where(low, core, 1 - core))
    unit(slots.at[2 * far + pick], True)
    finish(other)
    return_back(2 * far, other)

    send_sibling(0, own_ref).wait_recv()
    unit(slots.at[1], False)
    finish(sibling)

    def drain(hop, carry):
        send_left(hop, own_ref).wait_send()
        send_sibling(hop, own_ref).wait_send()
        return carry

    send_sibling(0, own_ref).wait_send()
    lax.fori_loop(1, far + 1, drain, 0)

    def drain_back(slot, carry):
        send_back(slot, sibling).wait()
        return carry

    lax.fori_loop(2, 2 * far + 1, drain_back, 0)


def pair_beams(packed, n, snake):
    stations, width = packed.shape
    segs = SEGS
    half = (width - LANES) // (2 * segs)
    far = n // 4
    dma = pltpu.SemaphoreType.DMA
    pairs = (n // 2 + 1) * stations * stations * half
    return pl.pallas_call(
        functools.partial(pair_kernel, n, snake),
        out_shape=jax.ShapeDtypeStruct((n, stations, 2 * half), jnp.bfloat16),
        in_specs=[pl.BlockSpec(memory_space=pltpu.VMEM)],
        out_specs=pl.BlockSpec(memory_space=pltpu.VMEM),
        scratch_shapes=[
            pltpu.VMEM((2 * far + 2, stations, width), jnp.bfloat16),
            pltpu.VMEM((stations, segs, ROWS, 3 * half + LANES), jnp.float32),
            pltpu.VMEM((segs, stations, 3 * half + LANES), jnp.float32),
            pltpu.VMEM((stations, ROWS, 2 * half), jnp.float32),
            pltpu.VMEM((stations, 2 * half), jnp.float32),
            pltpu.VMEM((2 * far + 1, stations, 2 * half), jnp.bfloat16),
            dma((far + 1,)), dma((far + 1,)), dma((far + 1,)), dma((far + 1,)),
            dma((2 * far + 1,)), dma((2 * far + 1,)),
        ],
        compiler_params=pltpu.CompilerParams(
            collective_id=0, has_side_effects=True, vmem_limit_bytes=48 * 1024 * 1024
        ),
        cost_estimate=pl.CostEstimate(
            flops=66 * pairs, bytes_accessed=2 * packed.size, transcendentals=0
        ),
        name="pair_beams",
    )(packed)


def shards(snake, spectra, counts):
    n = lax.axis_size("blk")
    stations, segs, spread = spectra.shape
    lanes = jnp.pad(counts.astype(jnp.bfloat16), ((0, 0), (0, LANES - segs)))
    packed = jnp.concatenate([spectra.reshape(stations, -1), lanes], 1)
    beams = pair_beams(packed, n, snake)
    table = lag_table()
    rows = jnp.dot(beams.reshape(-1, spread), table, preferred_element_type=jnp.float32)
    values = rows.astype(jnp.bfloat16).astype(jnp.float32)
    scale = jnp.sqrt(jnp.mean(values * values, -1, keepdims=True) + 1e-06)
    out = (values / scale).astype(jnp.bfloat16)
    return out.reshape(n, stations, LAG).transpose(1, 0, 2)


def solution(mesh):
    snake = mesh.shape["blk"] == 16
    return jax.shard_map(
        functools.partial(shards, snake),
        mesh=mesh,
        in_specs=(P(("band", "blk"), None, None), P(("band", "blk"), None)),
        out_specs=P(("band", "blk"), None, None),
        check_vma=False,
    )
```
